32 devices in a mesh: grp: 2 (over y), freq: 8 (over z, x), site: 2 (over core).
Axes of the slice: x: 2, y: 2, z: 4, core: 2. Of those that a mesh axis runs over, the one named last changes fastest.
Arguments:
- green: bfloat16 [8, 1024, 8, 3, 2, 128], P('freq', None, ('grp', 'site')), parts along dimension 2, may hold values from -0.1875 to 0.1875
- slip: bfloat16 [8, 16, 8, 128], P(None, 'site'), may hold values from 0.099609375 to 1
- positions: float32 [3, 1024], replicated, may hold values from 0 to 40
- hypocenters: float32 [8, 4, 3], replicated, may hold values from 0 to 40
- slowness: float32 [8, 4], replicated, may hold values from 1 to 3
- rise: float32 [8, 16], replicated, may hold values from 0.5 to 6
- block_lists: int32 [8, 8], replicated, may hold values from 0 to 7, as said below
- block_counts: int32 [8], replicated, may hold values from 1 to 8, 48 in all
- var_counts: int32 [8], replicated, may hold values from 1 to 64, as said below
- region_map: int32 [8], replicated, may hold values from 0 to 7, each once
Outputs:
- seismograms: float32 [512, 8, 3, 2048], P('freq', ('grp', 'site')), parts along dimension 1
The draws below stay inside these ranges and needn't reach their ends.
There are 2 independent parts, one for each index of `grp`. The reference program is written for one: setup_inputs(seed, part) draws one part's arguments, and reference() takes and returns one part's arrays. A program takes and returns all parts, laid end to end along the dimension named above; an argument that names none is the same for every part. Nothing has to cross between parts.
Inputs may be any that keep to these rules, and one draw needn't show every extreme that they name: `block_lists`: rupture r lists consecutive blocks s_r, s_r + 1, ... modulo 8; only its first block_counts[r] entries are used. `block_counts`: the counts sum to 48. Variations 0 .. var_counts[r] - 1 of rupture r are live. `region_map`: each row appears once.
All inputs are finite; a program needn't handle non-finite values.
Results may differ from the reference program's by a relative error of at most 0.0048.
Values may be sent and summed in bfloat16 or wider, within the bound.
A program may use at most 192 MiB of HBM per device.

```python
import math
import jax
import jax.numpy as jnp
import numpy as np
from jax import lax

F = 1024
PB = 128
NB = 8
SITES = 4
C = 3
K = 16
H = 4
VARS = 64
R = 8
LMAX = 8
TOTAL_BLK = 48


def draw_block_lists(key, part):
    starts = jax.random.randint(key, (R,), 0, NB, dtype=jnp.int32)
    starts = starts.at[0].set(NB - 1)
    offsets = jnp.arange(LMAX, dtype=jnp.int32)
    return ((starts[:, None] + offsets[None, :]) % NB).astype(jnp.int32)


def draw_var_counts(key, part):
    first_key = jax.random.fold_in(key, 11)
    second_key = jax.random.fold_in(key, 12)
    counts = jax.random.randint(first_key, (R,), 1, VARS + 1, dtype=jnp.int32)
    chosen = jax.random.randint(second_key, (), 0, R, dtype=jnp.int32)
    return counts.at[chosen].set(VARS).astype(jnp.int32)


def shard_levels(key, dims, split, low, top_value):
    level, own = 1.0, jax.random.fold_in(key, 6)
    for axis_at, shards_of in split:
        draws = jnp.exp(jax.random.uniform(jax.random.fold_in(own, axis_at), (shards_of,), jnp.float32, low / len(split), top_value / len(split)))
        level = level * jnp.repeat(draws, dims[axis_at] // shards_of).reshape([-1 if axis == axis_at else 1 for axis in range(len(dims))])
    return level


def split_up(number_of, total, reach, lean):
    portions = [(1 << 20) // math.isqrt(rank ** lean) + 1 for rank in range(2, number_of + 1)]
    spare, given = total - reach - (number_of - 1), [1] * (number_of - 1)
    while spare > 0:
        movable = [i for i in range(number_of - 1) if given[i] < reach]
        whole, budget = sum([portions[i] for i in movable]), spare
        for i in movable:
            addition = min(reach - given[i], max(1, budget * portions[i] // whole), spare)
            given[i] = given[i] + addition
            spare = spare - addition
    return np.array([reach] + given)


def ragged_sizes(key, number_of, total, limit, slope):
    if number_of == 2:
        one = jax.random.randint(key, (), max(1, total - limit), min(limit, total - 1) + 1)
        return jnp.stack([one, total - one])
    sizes = jnp.asarray(split_up(number_of, total, limit, slope), jnp.int32)
    couples = (number_of - 1) // 2
    giver, taker = sizes[1:1 + 2 * couples:2], sizes[2:2 + 2 * couples:2]
    margin = jnp.minimum(giver - 1, limit - taker)
    shifted = jax.random.randint(jax.random.fold_in(key, 1), (couples,), 0, 1 << 20) % (margin + 1)
    sizes = sizes.at[1:1 + 2 * couples:2].set(giver - shifted).at[2:2 + 2 * couples:2].set(taker + shifted)
    return sizes[jax.random.permutation(jax.random.fold_in(key, 2), number_of)]


def gaussian(rng, extent, width, most, pieces=(), held_as=jnp.bfloat16):
    values = width * jax.random.normal(rng, extent, jnp.float32)
    if pieces:
        values = values * shard_levels(rng, extent, pieces, -0.22, 0.18)
    return jnp.clip(values, -most, most).astype(held_as)


def setup_inputs(seed: int = 0, part: int = 0) -> dict:
    splits = jax.random.split(jax.random.key(seed), 11)
    own_keys = jax.random.split(jax.random.fold_in(splits[10], part), 11)
    return {
        "green": gaussian(own_keys[0], (NB, F, SITES, C, 2, PB), (LMAX * PB) ** -0.5, 0.1875, ((0, 8), (2, 2))),
        "slip": jnp.clip(jnp.exp(math.log(1.0) - 2.306499 * jax.random.uniform(splits[1], (R, K, LMAX, PB), jnp.float32) ** shard_levels(splits[1], (R, K, LMAX, PB), ((1, 2),), -0.2, 0.2)), 0.099609375, 1.0).astype(jnp.bfloat16),
        "positions": jnp.clip(jax.random.uniform(splits[2], (3, NB * PB), jnp.float32, 0.0, 40.0), 0.0, 40.0),
        "hypocenters": jnp.clip(jax.random.uniform(splits[3], (R, H, 3), jnp.float32, 0.0, 40.0), 0.0, 40.0),
        "slowness": jnp.clip(jnp.exp(jax.random.uniform(splits[4], (R, H), jnp.float32, math.log(1.0), math.log(3.0))), 1.0, 3.0),
        "rise": jnp.clip(jnp.exp(jax.random.uniform(splits[5], (R, K), jnp.float32, math.log(0.5), math.log(6.0))), 0.5, 6.0),
        "block_lists": draw_block_lists(jax.random.fold_in(splits[10], 71), part),
        "block_counts": ragged_sizes(splits[7], R, TOTAL_BLK, LMAX, 2).astype(jnp.int32),
        "var_counts": draw_var_counts(jax.random.fold_in(splits[10], 71), part),
        "region_map": jax.random.permutation(splits[9], NB).astype(jnp.int32),
    }


TWO_PI = 2.0 * math.pi
OUT_GAIN = 8.0

def reference(green, slip, positions, hypocenters, slowness, rise, block_lists, block_counts, var_counts, region_map):
    wave_len = 2 * F
    omegas = TWO_PI * jnp.arange(F, dtype=jnp.int32).astype(jnp.float32) / wave_len
    points_all = positions.reshape(3, NB, PB)

    def rupture_spectrum(rupture):
        centers = hypocenters[rupture]
        slows = slowness[rupture]

        def add_block(totals, place):
            block = block_lists[rupture, place]
            tile = green[region_map[block]].astype(jnp.float32)
            points = points_all[:, block, :]
            sq_dist = lax.optimization_barrier(jnp.sum((points[None, :, :] - centers[:, :, None]) ** 2, axis=1))
            onset_time = slows[:, None] * jnp.sqrt(sq_dist)
            phases = omegas[None, :, None] * onset_time[:, None, :]
            wave_re = jnp.cos(phases)[:, :, None, None, :]
            wave_im = -jnp.sin(phases)[:, :, None, None, :]
            tile_re = tile[None, :, :, :, 0, :]
            tile_im = tile[None, :, :, :, 1, :]
            weighted = jnp.stack([wave_re * tile_re - wave_im * tile_im, wave_re * tile_im + wave_im * tile_re], axis=4).astype(jnp.bfloat16)
            amps = slip[rupture, :, place, :]
            amps = jnp.where(place < block_counts[rupture], amps, jnp.zeros_like(amps))
            term = jnp.einsum('kp,hfscqp->khfscq', amps.astype(jnp.float32), weighted.astype(jnp.float32))
            return (totals + term, None)
        start_totals = jnp.zeros((K, H, F, SITES, C, 2), jnp.float32)
        totals, _ = lax.scan(add_block, start_totals, jnp.arange(LMAX, dtype=jnp.int32))
        ratio = omegas[None, :] * rise[rupture][:, None]
        denom = 1.0 + ratio * ratio
        stf_re = (1.0 / denom)[:, None, :, None, None]
        stf_im = (-ratio / denom)[:, None, :, None, None]
        part_re = totals[..., 0]
        part_im = totals[..., 1]
        spec_re = stf_re * part_re - stf_im * part_im
        spec_im = stf_re * part_im + stf_im * part_re
        spectrum = jnp.stack([spec_re, spec_im], axis=-1).transpose(0, 1, 3, 4, 5, 2)
        variation = jnp.arange(K, dtype=jnp.int32)[:, None] * H + jnp.arange(H, dtype=jnp.int32)[None, :]
        live = variation < var_counts[rupture]
        spectrum = jnp.where(live[:, :, None, None, None, None], spectrum, jnp.zeros_like(spectrum))
        return spectrum.reshape(VARS, SITES, C, 2, F).astype(jnp.bfloat16)
    spectra = lax.map(rupture_spectrum, jnp.arange(R, dtype=jnp.int32))
    spec_rows = spectra.reshape(R * VARS * SITES * C, 2 * F)
    bins = jnp.arange(F, dtype=jnp.int32)
    samples = jnp.arange(wave_len, dtype=jnp.int32)
    products = bins[:, None] * samples[None, :] % wave_len
    angles = TWO_PI * products.astype(jnp.float32) / wave_len
    wave_table = jnp.concatenate([jnp.cos(angles), -jnp.sin(angles)], axis=0).astype(jnp.bfloat16)
    motion = jnp.dot(spec_rows, wave_table, preferred_element_type=jnp.float32) * (OUT_GAIN / math.sqrt(F))
    return motion.reshape(R * VARS, SITES, C, wave_len)
```

```python
import math

import jax
import jax.numpy as jnp
from jax import lax
from jax.experimental import pallas as pl
from jax.experimental.pallas import tpu as pltpu
from jax.sharding import PartitionSpec as P

F = 1024
C = 3


TWO_PI = 2.0 * math.pi
OUT_GAIN = 8.0
LANES = 128

SIN_COEFS = tuple((-1) ** i * math.pi ** (2 * i + 1) / math.factorial(2 * i + 1) for i in range(7))
COS_COEFS = tuple((-1) ** i * math.pi ** (2 * i) / math.factorial(2 * i) for i in range(7))


def turn_waves(turns):
    frac = turns - jnp.round(turns)
    square = frac * frac
    half_sin = SIN_COEFS[-1]
    for coef in SIN_COEFS[-2::-1]:
        half_sin = half_sin * square + coef
    half_sin = half_sin * frac
    half_cos = COS_COEFS[-1]
    for coef in COS_COEFS[-2::-1]:
        half_cos = half_cos * square + coef
    return 1.0 - 2.0 * half_sin * half_sin, 2.0 * half_sin * half_cos


def synth_kernel(
    lists,
    counts,
    var_counts,
    regions,
    first_bin,
    centers,
    slows,
    tiles,
    slip,
    points,
    rise,
    out,
    cos_buf,
    sin_buf,
    total,
):
    rup = pl.program_id(0)
    sites, bins = tiles.shape[1], tiles.shape[4]
    real_count = slip.shape[1]
    list_len = slip.shape[0] // pl.num_programs(0)
    hypo_count = cos_buf.shape[0] * 2
    step = 16
    start = first_bin[0]
    total[...] = jnp.zeros_like(total)

    def one_slot(place, carry):
        block = lists[rup * list_len + place]
        region = regions[block]
        xyz = points[block]
        low = lax.broadcasted_iota(jnp.int32, (step, LANES), 0).astype(jnp.float32)
        high = (start + step * lax.broadcasted_iota(jnp.int32, (bins // step, LANES), 0)).astype(
            jnp.float32
        )
        for hypo in range(hypo_count):
            at = (rup * hypo_count + hypo) * 3
            sq_dist = jnp.zeros((1, LANES), jnp.float32)
            for axis in range(3):
                gap = xyz[axis : axis + 1, :] - centers[at + axis]
                sq_dist = sq_dist + gap * gap
            onset = slows[rup * hypo_count + hypo] * jnp.sqrt(sq_dist)
            rate = onset * (1.0 / (2 * F))
            low_cos, low_sin = turn_waves(low * rate)
            high_cos, high_sin = turn_waves(high * rate)
            lane = (hypo % 2) * LANES
            for part in range(bins // step):
                hc, hs = high_cos[part : part + 1], high_sin[part : part + 1]
                cos = (hc * low_cos - hs * low_sin).astype(jnp.bfloat16)
                sin = (hs * low_cos + hc * low_sin).astype(jnp.bfloat16)
                rows = pl.ds(part * step, step)
                cos_buf[hypo // 2, rows, lane : lane + LANES] = cos
                sin_buf[hypo // 2, rows, lane : lane + LANES] = sin
        amps = slip[rup * list_len + place]
        none = jnp.zeros_like(amps)
        paired = jnp.concatenate(
            [jnp.concatenate([amps, none], axis=1), jnp.concatenate([none, amps], axis=1)], axis=0
        )
        for site in range(sites):
            for comp in range(C):
                tile_re = tiles[region, site, comp, 0]
                tile_im = tiles[region, site, comp, 1]
                tile_re = jnp.concatenate([tile_re, tile_re], axis=1)
                tile_im = jnp.concatenate([tile_im, tile_im], axis=1)
                for pair in range(hypo_count // 2):
                    cos, sin = cos_buf[pair], sin_buf[pair]
                    weighted = jnp.concatenate(
                        [cos * tile_re + sin * tile_im, cos * tile_im - sin * tile_re], axis=0
                    )
                    total[site, comp, pair] += lax.dot_general(
                        paired,
                        weighted,
                        (((1,), (1,)), ((), ())),
                        preferred_element_type=jnp.float32,
                    )
        return carry

    lax.fori_loop(0, counts[rup], one_slot, 0)
    omegas = (start + lax.broadcasted_iota(jnp.int32, (real_count, bins), 1)).astype(
        jnp.float32
    ) * (TWO_PI / (2 * F))
    ratio = omegas * rise[0]
    stf_re = 1.0 / (1.0 + ratio * ratio)
    stf_im = -ratio * stf_re
    reals = lax.broadcasted_iota(jnp.int32, (real_count, bins), 0)
    for pair in range(hypo_count // 2):
        for side in range(2):
            hypo = pair * 2 + side
            live = reals * hypo_count + hypo < var_counts[rup]
            rows = slice(side * real_count, (side + 1) * real_count)
            kept = slice(hypo * real_count, (hypo + 1) * real_count)
            for site in range(sites):
                for comp in range(C):
                    part_re = total[site, comp, pair, rows, :bins]
                    part_im = total[site, comp, pair, rows, bins:]
                    spec_re = stf_re * part_re - stf_im * part_im
                    spec_im = stf_re * part_im + stf_im * part_re
                    out[0, site, comp, 0, kept] = jnp.where(live, spec_re, 0.0).astype(out.dtype)
                    out[0, site, comp, 1, kept] = jnp.where(live, spec_im, 0.0).astype(out.dtype)


def synthesize(tiles, slip, points, rise, scalars, hypo_count):
    rupture_count = rise.shape[0]
    real_count = rise.shape[1]
    _, sites, _, _, bins, _ = tiles.shape
    whole = pl.BlockSpec(memory_space=pltpu.VMEM)
    return pl.pallas_call(
        synth_kernel,
        grid_spec=pltpu.PrefetchScalarGridSpec(
            num_scalar_prefetch=len(scalars),
            grid=(rupture_count,),
            in_specs=[
                whole,
                whole,
                whole,
                pl.BlockSpec((1, real_count, bins), lambda r, *_: (r, 0, 0)),
            ],
            out_specs=pl.BlockSpec(
                (1, sites, C, 2, hypo_count * real_count, bins),
                lambda r, *_: (r, 0, 0, 0, 0, 0),
            ),
            scratch_shapes=[
                pltpu.VMEM((hypo_count // 2, bins, 2 * LANES), jnp.bfloat16),
                pltpu.VMEM((hypo_count // 2, bins, 2 * LANES), jnp.bfloat16),
                pltpu.VMEM((sites, C, hypo_count // 2, 2 * real_count, 2 * bins), jnp.float32),
            ],
        ),
        out_shape=jax.ShapeDtypeStruct(
            (rupture_count, sites, C, 2, hypo_count * real_count, bins), jnp.bfloat16
        ),
        compiler_params=pltpu.CompilerParams(dimension_semantics=("arbitrary",)),
        cost_estimate=pl.CostEstimate(
            flops=sites * 2 * 10**10, bytes_accessed=4 * 10**7, transcendentals=0
        ),
    )(*scalars, tiles, slip, points, rise)


def make_wave_table():
    wave_len = 2 * F
    chunk = LANES
    bins = jnp.arange(F, dtype=jnp.int32)[:, None]

    def waves(samples):
        angles = TWO_PI / wave_len * (bins * samples[None, :] % wave_len).astype(jnp.float32)
        return jnp.cos(angles), jnp.sin(angles)

    low_cos, low_sin = waves(jnp.arange(chunk, dtype=jnp.int32))
    high_cos, high_sin = waves(jnp.arange(wave_len // chunk, dtype=jnp.int32) * chunk)
    low_cos, low_sin = low_cos[:, None, :], low_sin[:, None, :]
    high_cos, high_sin = high_cos[:, :, None], high_sin[:, :, None]
    cos = (high_cos * low_cos - high_sin * low_sin).astype(jnp.bfloat16)
    sin = (high_sin * low_cos + high_cos * low_sin).astype(jnp.bfloat16)
    return jnp.stack([cos, -sin]).reshape(2 * F, wave_len)


def on_device(
    green,
    slip,
    positions,
    hypocenters,
    slowness,
    rise,
    block_lists,
    block_counts,
    var_counts,
    region_map,
):
    freq_count = lax.axis_size("freq")
    site_shards = lax.axis_size("site")
    fdev_bins = green.shape[1] // freq_count
    point_count = green.shape[-1]
    rupture_count, list_len = block_lists.shape
    hypo_count = hypocenters.shape[1]
    wave_len = 2 * F
    block_total = positions.shape[1] // point_count
    pieces = [slip]
    for shift in range(1, site_shards):
        pieces.append(
            lax.ppermute(
                slip, "site", [(i, (i - shift) % site_shards) for i in range(site_shards)]
            )
        )
    ring = jnp.stack(pieces)
    own = lax.axis_index("site")
    order = (jnp.arange(site_shards) - own) % site_shards
    slip_all = ring[order].transpose(1, 3, 0, 2, 4)
    real_count = site_shards * slip.shape[1]
    slip_all = slip_all.reshape(rupture_count * list_len, real_count, point_count)
    points = positions.reshape(3, block_total, point_count).transpose(1, 0, 2)
    first_bin = (lax.axis_index("freq") * fdev_bins).astype(jnp.int32).reshape(1)
    scalars = (
        block_lists.reshape(-1),
        block_counts,
        var_counts,
        region_map,
        first_bin,
        hypocenters.reshape(-1),
        slowness.reshape(-1),
    )
    rise_rows = jnp.broadcast_to(rise[:, :, None], (rupture_count, real_count, fdev_bins))
    site_items = green.shape[2]
    rows_here, _, _, comps, _, _ = green.shape
    wave_table = make_wave_table()
    motions = []
    for site in range(site_items):
        piece = green[:, :, site : site + 1].reshape(
            rows_here, freq_count, fdev_bins, 1, comps, 2, point_count
        )
        piece = piece.transpose(1, 0, 3, 4, 5, 2, 6)
        tiles = lax.all_to_all(piece, "freq", split_axis=0, concat_axis=0, tiled=True)
        tiles = tiles.reshape(freq_count * rows_here, 1, comps, 2, fdev_bins, point_count)
        spectrum = synthesize(tiles, slip_all, points, rise_rows, scalars, hypo_count)
        own_rows = lax.all_to_all(spectrum, "freq", split_axis=0, concat_axis=0, tiled=True)
        own_rows = own_rows.reshape(
            freq_count, rupture_count // freq_count, comps, 2, hypo_count, real_count, fdev_bins
        ).transpose(1, 5, 4, 2, 3, 0, 6)
        row_count = rupture_count // freq_count * hypo_count * real_count
        spec_rows = own_rows.reshape(row_count * comps, wave_len)
        motion = jnp.dot(spec_rows, wave_table, preferred_element_type=jnp.float32) * (
            OUT_GAIN / math.sqrt(F)
        )
        motions.append(motion.reshape(row_count, 1, comps, wave_len))
    return jnp.concatenate(motions, axis=1)


def on_device_small(
    green,
    slip,
    positions,
    hypocenters,
    slowness,
    rise,
    block_lists,
    block_counts,
    var_counts,
    region_map,
):
    freq_count = lax.axis_size("freq")
    fdev_bins = green.shape[1] // freq_count
    point_count = green.shape[-1]
    rupture_count = block_lists.shape[0]
    list_len = block_lists.shape[1]
    hypo_count = hypocenters.shape[1]
    wave_len = 2 * F
    slip_all = lax.all_gather(slip, "site", axis=1, tiled=True)
    real_count = slip_all.shape[1]
    first_bin = lax.axis_index("freq") * fdev_bins
    local_bins = first_bin + jnp.arange(fdev_bins, dtype=jnp.int32)
    omegas = TWO_PI * local_bins.astype(jnp.float32) / wave_len
    points_all = positions.reshape(3, positions.shape[1] // point_count, point_count)
    slot_total = rupture_count * list_len
    slot_index = jnp.arange(slot_total, dtype=jnp.int32)
    slot_rup = slot_index // list_len
    slot_pos = slot_index % list_len
    slot_live = slot_pos < block_counts[slot_rup]
    group_size = math.gcd(slot_total, 32)
    turn_count = slot_total // group_size
    rupture_ids = jnp.arange(rupture_count, dtype=jnp.int32)
    tiles_here = lax.all_to_all(green, "freq", split_axis=1, concat_axis=0, tiled=True)
    site_items = tiles_here.shape[2]

    def one_turn(turn_index, totals):
        start = turn_index * group_size
        group_rup = lax.dynamic_slice_in_dim(slot_rup, start, group_size)
        group_pos = lax.dynamic_slice_in_dim(slot_pos, start, group_size)
        group_live = lax.dynamic_slice_in_dim(slot_live, start, group_size)
        blocks = block_lists[group_rup, group_pos]
        tile = tiles_here[region_map[blocks]].astype(jnp.float32)
        points = points_all[:, blocks, :].transpose(1, 0, 2)
        centers = hypocenters[group_rup]
        slows = slowness[group_rup]
        sq_dist = jnp.sum((points[:, None, :, :] - centers[:, :, :, None]) ** 2, axis=2)
        onset_time = slows[:, :, None] * jnp.sqrt(sq_dist)
        phases = omegas[None, None, :, None] * onset_time[:, :, None, :]
        wave_re = jnp.cos(phases)[:, :, :, None, None, :]
        wave_im = -jnp.sin(phases)[:, :, :, None, None, :]
        tile_re = tile[:, None, :, :, :, 0, :]
        tile_im = tile[:, None, :, :, :, 1, :]
        weighted = jnp.stack(
            [wave_re * tile_re - wave_im * tile_im, wave_re * tile_im + wave_im * tile_re], axis=5
        ).astype(jnp.bfloat16)
        amps = slip_all[group_rup, :, group_pos]
        amps = jnp.where(group_live[:, None, None], amps, jnp.zeros_like(amps))
        onehot = (group_rup[None, :] == rupture_ids[:, None]).astype(jnp.bfloat16)
        routed = onehot[:, :, None, None] * amps[None, :, :, :]
        term = jnp.einsum(
            "rgkp,ghfscqp->rkhfscq", routed, weighted, preferred_element_type=jnp.float32
        )
        return totals + term

    start_totals = jnp.zeros(
        (rupture_count, real_count, hypo_count, fdev_bins, site_items, C, 2), jnp.float32
    )
    totals = lax.fori_loop(0, turn_count, one_turn, start_totals)
    ratio = omegas[None, None, :] * rise[:, :, None]
    denom = 1.0 + ratio * ratio
    stf_re = (1.0 / denom)[:, :, None, :, None, None]
    stf_im = (-ratio / denom)[:, :, None, :, None, None]
    part_re = totals[..., 0]
    part_im = totals[..., 1]
    spec_re = stf_re * part_re - stf_im * part_im
    spec_im = stf_re * part_im + stf_im * part_re
    spectrum = jnp.stack([spec_re, spec_im], axis=-1).transpose(0, 1, 2, 4, 5, 6, 3)
    variation = (
        jnp.arange(real_count, dtype=jnp.int32)[:, None] * hypo_count
        + jnp.arange(hypo_count, dtype=jnp.int32)[None, :]
    )
    live = variation[None, :, :] < var_counts[:, None, None]
    spectrum = jnp.where(live[:, :, :, None, None, None, None], spectrum, jnp.zeros_like(spectrum))
    spectrum = spectrum.reshape(
        rupture_count * real_count * hypo_count, site_items, C, 2, fdev_bins
    ).astype(jnp.bfloat16)
    own_rows = lax.all_to_all(spectrum, "freq", split_axis=0, concat_axis=4, tiled=True)
    row_count = own_rows.shape[0]
    site_count = own_rows.shape[1]
    spec_rows = own_rows.reshape(row_count * site_count * C, 2 * F)
    bins = jnp.arange(F, dtype=jnp.int32)
    piece_len = min(512, wave_len)
    pieces = []
    for piece_index in range(wave_len // piece_len):
        samples = piece_index * piece_len + jnp.arange(piece_len, dtype=jnp.int32)
        products = bins[:, None] * samples[None, :] % wave_len
        angles = TWO_PI * products.astype(jnp.float32) / wave_len
        wave_table = jnp.concatenate([jnp.cos(angles), -jnp.sin(angles)], axis=0).astype(
            jnp.bfloat16
        )
        pieces.append(
            jnp.dot(spec_rows, wave_table, preferred_element_type=jnp.float32)
            * (OUT_GAIN / math.sqrt(F))
        )
    motion = jnp.concatenate(pieces, axis=1)
    return motion.reshape(row_count, site_count, C, wave_len)


def on_device_any(green, slip, positions, hypocenters, *rest):
    freq_count = lax.axis_size("freq")
    fdev_bins = green.shape[1] // freq_count
    rupture_count, hypo_count = hypocenters.shape[:2]
    lanes_fit = fdev_bins == LANES and green.shape[-1] == LANES
    if lanes_fit and hypo_count % 2 == 0 and rupture_count % freq_count == 0:
        return on_device(green, slip, positions, hypocenters, *rest)
    return on_device_small(green, slip, positions, hypocenters, *rest)


def solution(mesh):
    placed = (
        P("freq", None, ("grp", "site"), None, None, None),
        P(None, "site", None, None),
        P(),
        P(),
        P(),
        P(),
        P(),
        P(),
        P(),
        P(),
    )
    return jax.shard_map(
        on_device_any,
        mesh=mesh,
        in_specs=placed,
        out_specs=P("freq", ("grp", "site"), None, None),
        check_vma=False,
    )
```

```python
import math

import jax
import jax.numpy as jnp
from jax import lax
from jax.experimental import pallas as pl
from jax.experimental.pallas import tpu as pltpu
from jax.sharding import PartitionSpec as P


F = 1024
C = 3


TWO_PI = 2.0 * math.pi
OUT_GAIN = 8.0
LANES = 128

SIN_COEFS = tuple((-1) ** i * math.pi ** (2 * i + 1) / math.factorial(2 * i + 1) for i in range(7))
COS_COEFS = tuple((-1) ** i * math.pi ** (2 * i) / math.factorial(2 * i) for i in range(7))


def turn_waves(turns):
    frac = turns - jnp.round(turns)
    square = frac * frac
    half_sin = SIN_COEFS[-1]
    for coef in SIN_COEFS[-2::-1]:
        half_sin = half_sin * square + coef
    half_sin = half_sin * frac
    half_cos = COS_COEFS[-1]
    for coef in COS_COEFS[-2::-1]:
        half_cos = half_cos * square + coef
    return 1.0 - 2.0 * half_sin * half_sin, 2.0 * half_sin * half_cos


def wave_kernel(lists, counts, first_bin, centers, slows, points, cos_out, sin_out):
    rup = pl.program_id(0)
    _, list_len, pairs, bins, _ = cos_out.shape
    hypo_count = pairs * 2
    step = 16
    start = first_bin[0]

    def one_slot(place, carry):
        xyz = points[lists[rup * list_len + place]]
        low = lax.broadcasted_iota(jnp.int32, (step, LANES), 0).astype(jnp.float32)
        high = (start + step * lax.broadcasted_iota(jnp.int32, (bins // step, LANES), 0)).astype(
            jnp.float32
        )
        for hypo in range(hypo_count):
            at = (rup * hypo_count + hypo) * 3
            sq_dist = jnp.zeros((1, LANES), jnp.float32)
            for axis in range(3):
                gap = xyz[axis : axis + 1, :] - centers[at + axis]
                sq_dist = sq_dist + gap * gap
            onset = slows[rup * hypo_count + hypo] * jnp.sqrt(sq_dist)
            rate = onset * (1.0 / (2 * F))
            low_cos, low_sin = turn_waves(low * rate)
            high_cos, high_sin = turn_waves(high * rate)
            lane = (hypo % 2) * LANES
            for part in range(bins // step):
                hc, hs = high_cos[part : part + 1], high_sin[part : part + 1]
                cos = (hc * low_cos - hs * low_sin).astype(jnp.bfloat16)
                sin = (hs * low_cos + hc * low_sin).astype(jnp.bfloat16)
                rows = slice(part * step, (part + 1) * step)
                cos_out[0, place, hypo // 2, rows, lane : lane + LANES] = cos
                sin_out[0, place, hypo // 2, rows, lane : lane + LANES] = sin
        return carry

    lax.fori_loop(0, counts[rup], one_slot, 0)


def make_waves(points, scalars, rupture_count, list_len, hypo_count, bins):
    block = (1, list_len, hypo_count // 2, bins, 2 * LANES)
    shape = jax.ShapeDtypeStruct((rupture_count,) + block[1:], jnp.bfloat16)
    spec = pl.BlockSpec(block, lambda r, *_: (r, 0, 0, 0, 0))
    return pl.pallas_call(
        wave_kernel,
        grid_spec=pltpu.PrefetchScalarGridSpec(
            num_scalar_prefetch=len(scalars),
            grid=(rupture_count,),
            in_specs=[pl.BlockSpec(memory_space=pltpu.VMEM)],
            out_specs=[spec, spec],
        ),
        out_shape=[shape, shape],
        compiler_params=pltpu.CompilerParams(dimension_semantics=("arbitrary",)),
        cost_estimate=pl.CostEstimate(flops=10**6, bytes_accessed=10**5, transcendentals=0),
    )(*scalars, points)


def synth_kernel(
    lists, counts, var_counts, regions, first_bin, tiles, slip, cos_in, sin_in, rise, out, total
):
    rup = pl.program_id(0)
    sites, bins = tiles.shape[1], tiles.shape[4]
    _, list_len, pairs, _, _ = cos_in.shape
    real_count = slip.shape[1]
    hypo_count = pairs * 2
    start = first_bin[0]
    total[...] = jnp.zeros_like(total)

    def one_slot(place, carry):
        slot = rup * list_len + place
        region = regions[lists[slot]]
        amps = slip[slot]
        none = jnp.zeros_like(amps)
        paired = jnp.concatenate(
            [jnp.concatenate([amps, none], axis=1), jnp.concatenate([none, amps], axis=1)], axis=0
        )
        for site in range(sites):
            for comp in range(C):
                tile_re = tiles[region, site, comp, 0]
                tile_im = tiles[region, site, comp, 1]
                tile_re = jnp.concatenate([tile_re, tile_re], axis=1)
                tile_im = jnp.concatenate([tile_im, tile_im], axis=1)
                for pair in range(pairs):
                    cos, sin = cos_in[0, place, pair], sin_in[0, place, pair]
                    weighted = jnp.concatenate(
                        [cos * tile_re + sin * tile_im, cos * tile_im - sin * tile_re], axis=0
                    )
                    total[site, comp, pair] += lax.dot_general(
                        paired,
                        weighted,
                        (((1,), (1,)), ((), ())),
                        preferred_element_type=jnp.float32,
                    )
        return carry

    lax.fori_loop(0, counts[rup], one_slot, 0)
    omegas = (start + lax.broadcasted_iota(jnp.int32, (real_count, bins), 1)).astype(
        jnp.float32
    ) * (TWO_PI / (2 * F))
    ratio = omegas * rise[0]
    stf_re = 1.0 / (1.0 + ratio * ratio)
    stf_im = -ratio * stf_re
    reals = lax.broadcasted_iota(jnp.int32, (real_count, bins), 0)
    for pair in range(hypo_count // 2):
        for side in range(2):
            hypo = pair * 2 + side
            live = reals * hypo_count + hypo < var_counts[rup]
            rows = slice(side * real_count, (side + 1) * real_count)
            kept = slice(hypo * real_count, (hypo + 1) * real_count)
            for site in range(sites):
                for comp in range(C):
                    part_re = total[site, comp, pair, rows, :bins]
                    part_im = total[site, comp, pair, rows, bins:]
                    spec_re = stf_re * part_re - stf_im * part_im
                    spec_im = stf_re * part_im + stf_im * part_re
                    out[0, site, comp, 0, kept] = jnp.where(live, spec_re, 0.0).astype(out.dtype)
                    out[0, site, comp, 1, kept] = jnp.where(live, spec_im, 0.0).astype(out.dtype)


def synthesize(tiles, slip, cos_waves, sin_waves, rise, scalars):
    rupture_count, real_count, _ = rise.shape
    _, sites, _, _, bins, _ = tiles.shape
    pairs = cos_waves.shape[2]
    rows = 2 * pairs * real_count
    wave_spec = pl.BlockSpec((1,) + cos_waves.shape[1:], lambda r, *_: (r, 0, 0, 0, 0))
    whole = pl.BlockSpec(memory_space=pltpu.VMEM)
    return pl.pallas_call(
        synth_kernel,
        grid_spec=pltpu.PrefetchScalarGridSpec(
            num_scalar_prefetch=len(scalars),
            grid=(rupture_count,),
            in_specs=[
                whole,
                whole,
                wave_spec,
                wave_spec,
                pl.BlockSpec((1, real_count, bins), lambda r, *_: (r, 0, 0)),
            ],
            out_specs=pl.BlockSpec(
                (1, sites, C, 2, rows, bins), lambda r, *_: (r, 0, 0, 0, 0, 0)
            ),
            scratch_shapes=[pltpu.VMEM((sites, C, pairs, 2 * real_count, 2 * bins), jnp.float32)],
        ),
        out_shape=jax.ShapeDtypeStruct((rupture_count, sites, C, 2, rows, bins), jnp.bfloat16),
        compiler_params=pltpu.CompilerParams(dimension_semantics=("arbitrary",)),
        cost_estimate=pl.CostEstimate(
            flops=sites * 2 * 10**10, bytes_accessed=4 * 10**7, transcendentals=0
        ),
    )(*scalars, tiles, slip, cos_waves, sin_waves, rise)


def table_kernel(out):
    rows, wave_len = out.shape[1:]
    period = wave_len // LANES
    first = pl.program_id(0) * rows
    bins = first + lax.broadcasted_iota(jnp.int32, (rows, LANES), 0)
    samples = lax.broadcasted_iota(jnp.int32, (rows, LANES), 1)
    turns = (bins * samples % wave_len).astype(jnp.float32) * (1.0 / wave_len)
    low_cos, low_sin = turn_waves(turns)
    residues = first + lax.broadcasted_iota(jnp.int32, (period, LANES), 0)
    for chunk in range(period):
        turns = (residues * chunk % period).astype(jnp.float32) * (1.0 / period)
        high_cos, high_sin = turn_waves(turns)
        lanes = slice(chunk * LANES, (chunk + 1) * LANES)
        for part in range(rows // period):
            here = slice(part * period, (part + 1) * period)
            lc, ls = low_cos[here], low_sin[here]
            out[0, here, lanes] = (high_cos * lc - high_sin * ls).astype(out.dtype)
            out[1, here, lanes] = (-(high_sin * lc + high_cos * ls)).astype(out.dtype)


def make_wave_table():
    wave_len = 2 * F
    rows = 128
    table = pl.pallas_call(
        table_kernel,
        grid=(F // rows,),
        out_specs=pl.BlockSpec((2, rows, wave_len), lambda i: (0, i, 0)),
        out_shape=jax.ShapeDtypeStruct((2, F, wave_len), jnp.bfloat16),
        compiler_params=pltpu.CompilerParams(dimension_semantics=("arbitrary",)),
        cost_estimate=pl.CostEstimate(flops=10**6, bytes_accessed=10**5, transcendentals=0),
    )()
    return table.reshape(2 * F, wave_len)


def rows_to_motion(spectra, table):
    freq_count, _, comps, _, _, _ = spectra.shape
    lines = [
        jnp.concatenate(
            [spectra[f, 0, comp, part] for part in range(2) for f in range(freq_count)], axis=1
        )
        for comp in range(comps)
    ]
    return jnp.dot(
        jnp.concatenate(lines, axis=0), table[...], preferred_element_type=jnp.float32
    ) * (OUT_GAIN / math.sqrt(F))


def early_kernel(spectra, table, out):
    out[...] = rows_to_motion(spectra, table)


def last_kernel(spectra, table, *rest):
    early, out = rest[:-1], rest[-1]
    reals, hypos, comps, sites, _ = out.shape
    for site in range(sites):
        motion = early[site][...] if site < sites - 1 else rows_to_motion(spectra, table)
        for comp in range(comps):
            for hypo in range(hypos):
                first = (comp * hypos + hypo) * reals
                out[:, hypo, comp, site, :] = motion[first : first + reals]


def early_motion(spectra, table):
    _, _, comps, _, rows, _ = spectra.shape
    depth, wave_len = table.shape
    piece = 512
    return pl.pallas_call(
        early_kernel,
        grid=(wave_len // piece,),
        in_specs=[
            pl.BlockSpec(memory_space=pltpu.VMEM),
            pl.BlockSpec((depth, piece), lambda i: (0, i)),
        ],
        out_specs=pl.BlockSpec((comps * rows, piece), lambda i: (0, i)),
        out_shape=jax.ShapeDtypeStruct((comps * rows, wave_len), jnp.float32),
        compiler_params=pltpu.CompilerParams(dimension_semantics=("arbitrary",)),
        cost_estimate=pl.CostEstimate(flops=10**9, bytes_accessed=10**7, transcendentals=0),
    )(spectra, table)


def last_motion(spectra, table, early, real_count, hypo_count):
    _, _, comps, _, rows, _ = spectra.shape
    depth, wave_len = table.shape
    sites = len(early) + 1
    piece = 512
    return pl.pallas_call(
        last_kernel,
        grid=(wave_len // piece,),
        in_specs=[
            pl.BlockSpec(memory_space=pltpu.VMEM),
            pl.BlockSpec((depth, piece), lambda i: (0, i)),
        ]
        + [pl.BlockSpec((comps * rows, piece), lambda i: (0, i)) for _ in early],
        out_specs=pl.BlockSpec(
            (real_count, hypo_count, comps, sites, piece), lambda i: (0, 0, 0, 0, i)
        ),
        out_shape=jax.ShapeDtypeStruct(
            (real_count, hypo_count, comps, sites, wave_len), jnp.float32
        ),
        compiler_params=pltpu.CompilerParams(dimension_semantics=("arbitrary",)),
        cost_estimate=pl.CostEstimate(flops=10**9, bytes_accessed=10**7, transcendentals=0),
    )(spectra, table, *early)


def on_device(
    green,
    slip,
    positions,
    hypocenters,
    slowness,
    rise,
    block_lists,
    block_counts,
    var_counts,
    region_map,
):
    freq_count = lax.axis_size("freq")
    site_shards = lax.axis_size("site")
    fdev_bins = green.shape[1] // freq_count
    point_count = green.shape[-1]
    rupture_count, list_len = block_lists.shape
    hypo_count = hypocenters.shape[1]
    block_total = positions.shape[1] // point_count
    pieces = [slip]
    for shift in range(1, site_shards):
        pieces.append(
            lax.ppermute(
                slip, "site", [(i, (i - shift) % site_shards) for i in range(site_shards)]
            )
        )
    own = lax.axis_index("site")
    slots = []
    for shard in range(site_shards):
        piece = pieces[0]
        for shift in range(1, site_shards):
            piece = jnp.where((own + shift) % site_shards == shard, pieces[shift], piece)
        slots.append(piece)
    slip_all = jnp.concatenate(slots, axis=1).transpose(0, 2, 1, 3)
    real_count = slip_all.shape[2]
    slip_all = slip_all.reshape(rupture_count * list_len, real_count, point_count)
    points = positions.reshape(3, block_total, point_count).transpose(1, 0, 2)
    first_bin = (lax.axis_index("freq") * fdev_bins).astype(jnp.int32).reshape(1)
    lists = block_lists.reshape(-1)
    rise_rows = jnp.broadcast_to(rise[:, :, None], (rupture_count, real_count, fdev_bins))
    cos_waves, sin_waves = make_waves(
        points,
        (lists, block_counts, first_bin, hypocenters.reshape(-1), slowness.reshape(-1)),
        rupture_count,
        list_len,
        hypo_count,
        fdev_bins,
    )
    table = make_wave_table()
    site_items = green.shape[2]
    rows_here, _, _, comps, _, _ = green.shape
    scalars = (lists, block_counts, var_counts, region_map, first_bin)
    early = []
    for site in range(site_items):
        piece = green[:, :, site : site + 1].reshape(
            rows_here, freq_count, fdev_bins, 1, comps, 2, point_count
        )
        piece = piece.transpose(1, 0, 3, 4, 5, 2, 6)
        tiles = lax.all_to_all(piece, "freq", split_axis=0, concat_axis=0, tiled=True)
        tiles = tiles.reshape(freq_count * rows_here, 1, comps, 2, fdev_bins, point_count)
        spectrum = synthesize(tiles, slip_all, cos_waves, sin_waves, rise_rows, scalars)
        own_rows = lax.all_to_all(spectrum, "freq", split_axis=0, concat_axis=0, tiled=True)
        if site < site_items - 1:
            early.append(early_motion(own_rows, table))
        else:
            motion = last_motion(own_rows, table, early, real_count, hypo_count)
    motion = motion.reshape(real_count * hypo_count, comps, site_items, 2 * F)
    return motion.transpose(0, 2, 1, 3)


def on_device_small(
    green,
    slip,
    positions,
    hypocenters,
    slowness,
    rise,
    block_lists,
    block_counts,
    var_counts,
    region_map,
):
    freq_count = lax.axis_size("freq")
    fdev_bins = green.shape[1] // freq_count
    point_count = green.shape[-1]
    rupture_count = block_lists.shape[0]
    list_len = block_lists.shape[1]
    hypo_count = hypocenters.shape[1]
    wave_len = 2 * F
    slip_all = lax.all_gather(slip, "site", axis=1, tiled=True)
    real_count = slip_all.shape[1]
    first_bin = lax.axis_index("freq") * fdev_bins
    local_bins = first_bin + jnp.arange(fdev_bins, dtype=jnp.int32)
    omegas = TWO_PI * local_bins.astype(jnp.float32) / wave_len
    points_all = positions.reshape(3, positions.shape[1] // point_count, point_count)
    slot_total = rupture_count * list_len
    slot_index = jnp.arange(slot_total, dtype=jnp.int32)
    slot_rup = slot_index // list_len
    slot_pos = slot_index % list_len
    slot_live = slot_pos < block_counts[slot_rup]
    group_size = math.gcd(slot_total, 32)
    turn_count = slot_total // group_size
    rupture_ids = jnp.arange(rupture_count, dtype=jnp.int32)
    tiles_here = lax.all_to_all(green, "freq", split_axis=1, concat_axis=0, tiled=True)
    site_items = tiles_here.shape[2]

    def one_turn(turn_index, totals):
        start = turn_index * group_size
        group_rup = lax.dynamic_slice_in_dim(slot_rup, start, group_size)
        group_pos = lax.dynamic_slice_in_dim(slot_pos, start, group_size)
        group_live = lax.dynamic_slice_in_dim(slot_live, start, group_size)
        blocks = block_lists[group_rup, group_pos]
        tile = tiles_here[region_map[blocks]].astype(jnp.float32)
        points = points_all[:, blocks, :].transpose(1, 0, 2)
        centers = hypocenters[group_rup]
        slows = slowness[group_rup]
        sq_dist = jnp.sum((points[:, None, :, :] - centers[:, :, :, None]) ** 2, axis=2)
        onset_time = slows[:, :, None] * jnp.sqrt(sq_dist)
        phases = omegas[None, None, :, None] * onset_time[:, :, None, :]
        wave_re = jnp.cos(phases)[:, :, :, None, None, :]
        wave_im = -jnp.sin(phases)[:, :, :, None, None, :]
        tile_re = tile[:, None, :, :, :, 0, :]
        tile_im = tile[:, None, :, :, :, 1, :]
        weighted = jnp.stack(
            [wave_re * tile_re - wave_im * tile_im, wave_re * tile_im + wave_im * tile_re], axis=5
        ).astype(jnp.bfloat16)
        amps = slip_all[group_rup, :, group_pos]
        amps = jnp.where(group_live[:, None, None], amps, jnp.zeros_like(amps))
        onehot = (group_rup[None, :] == rupture_ids[:, None]).astype(jnp.bfloat16)
        routed = onehot[:, :, None, None] * amps[None, :, :, :]
        term = jnp.einsum(
            "rgkp,ghfscqp->rkhfscq", routed, weighted, preferred_element_type=jnp.float32
        )
        return totals + term

    start_totals = jnp.zeros(
        (rupture_count, real_count, hypo_count, fdev_bins, site_items, C, 2), jnp.float32
    )
    totals = lax.fori_loop(0, turn_count, one_turn, start_totals)
    ratio = omegas[None, None, :] * rise[:, :, None]
    denom = 1.0 + ratio * ratio
    stf_re = (1.0 / denom)[:, :, None, :, None, None]
    stf_im = (-ratio / denom)[:, :, None, :, None, None]
    part_re = totals[..., 0]
    part_im = totals[..., 1]
    spec_re = stf_re * part_re - stf_im * part_im
    spec_im = stf_re * part_im + stf_im * part_re
    spectrum = jnp.stack([spec_re, spec_im], axis=-1).transpose(0, 1, 2, 4, 5, 6, 3)
    variation = (
        jnp.arange(real_count, dtype=jnp.int32)[:, None] * hypo_count
        + jnp.arange(hypo_count, dtype=jnp.int32)[None, :]
    )
    live = variation[None, :, :] < var_counts[:, None, None]
    spectrum = jnp.where(live[:, :, :, None, None, None, None], spectrum, jnp.zeros_like(spectrum))
    spectrum = spectrum.reshape(
        rupture_count * real_count * hypo_count, site_items, C, 2, fdev_bins
    ).astype(jnp.bfloat16)
    own_rows = lax.all_to_all(spectrum, "freq", split_axis=0, concat_axis=4, tiled=True)
    row_count = own_rows.shape[0]
    site_count = own_rows.shape[1]
    spec_rows = own_rows.reshape(row_count * site_count * C, 2 * F)
    bins = jnp.arange(F, dtype=jnp.int32)
    piece_len = min(512, wave_len)
    pieces = []
    for piece_index in range(wave_len // piece_len):
        samples = piece_index * piece_len + jnp.arange(piece_len, dtype=jnp.int32)
        products = bins[:, None] * samples[None, :] % wave_len
        angles = TWO_PI * products.astype(jnp.float32) / wave_len
        wave_table = jnp.concatenate([jnp.cos(angles), -jnp.sin(angles)], axis=0).astype(
            jnp.bfloat16
        )
        pieces.append(
            jnp.dot(spec_rows, wave_table, preferred_element_type=jnp.float32)
            * (OUT_GAIN / math.sqrt(F))
        )
    motion = jnp.concatenate(pieces, axis=1)
    return motion.reshape(row_count, site_count, C, wave_len)


def on_device_any(green, slip, positions, hypocenters, *rest):
    freq_count = lax.axis_size("freq")
    fdev_bins = green.shape[1] // freq_count
    rupture_count, hypo_count = hypocenters.shape[:2]
    lanes_fit = fdev_bins == LANES and green.shape[-1] == LANES
    if lanes_fit and hypo_count % 2 == 0 and rupture_count == freq_count:
        return on_device(green, slip, positions, hypocenters, *rest)
    return on_device_small(green, slip, positions, hypocenters, *rest)


def solution(mesh):
    placed = (
        P("freq", None, ("grp", "site"), None, None, None),
        P(None, "site", None, None),
        P(),
        P(),
        P(),
        P(),
        P(),
        P(),
        P(),
        P(),
    )
    return jax.shard_map(
        on_device_any,
        mesh=mesh,
        in_specs=placed,
        out_specs=P("freq", ("grp", "site"), None, None),
        check_vma=False,
    )
```
